32 devices in a mesh: spot: 4 (over x, core), cell: 8 (over z, y).
Axes of the slice: x: 2, y: 2, z: 4, core: 2. Of those that a mesh axis runs over, the one named last changes fastest.
Arguments:
- logits: float32 [3, 4096, 2048], P(None, 'cell', 'spot'), may hold values from -8 to 8
- expression: float32 [3, 4096, 2048], P(None, 'cell', 'spot'), may hold values from 0.05 to 5
- measured: float32 [3, 2048, 2048], P(None, 'spot', 'cell'), may hold values from 0.05 to 5
- spot_slide: int32 [3, 2048], P(None, 'spot'), may hold values from 0 to 11, as said below
- cell_slide: int32 [3, 4096], P(None, 'cell'), may hold values from 0 to 11, as said below
- cell_valid: int32 [3, 4096], P(None, 'cell'), may hold values from 0 to 1, as said below
- gene_mask: int32 [12, 2048], replicated, may hold values from 0 to 1, as said below
Outputs:
- losses: float32 [3], replicated
- predicted: float32 [3, 2048, 2048], P(None, 'spot', 'cell')
- gene_cosine: float32 [3, 4, 2048], P(None, None, 'cell')
- spot_cosine: float32 [3, 2048], P(None, 'spot')
- logit_grad: float32 [3, 4096, 2048], P(None, 'cell', 'spot')
- expression_grad: float32 [3, 4096, 2048], P(None, 'cell', 'spot')
The draws below stay inside these ranges and needn't reach their ends.
Inputs may be any that keep to these rules, and one draw needn't show every extreme that they name: `spot_slide`: in micro-batch b the values lie in b * 4 to (b + 1) * 4 - 1 and never fall along spots; every such slide holds 128 spots or more. `cell_slide`: in micro-batch b the values lie in b * 4 to (b + 1) * 4 - 1 and never fall along cell slots; every such slide holds 256 slots or more. `cell_valid`: the first slot of every slide is valid. `gene_mask`: every slide measures at least one gene.
All inputs are finite; a program needn't handle non-finite values.
Results may differ from the reference program's by a relative error of at most 0.0003.
Values sent between devices are 32-bit elements; how exact they have to be, the bound alone decides.
No kernel may reach another device: no remote copies, remote signals or barrier semaphores. Data moves between devices by JAX's collectives and lax.ppermute only.
A program may use at most 192 MiB of HBM per device.

```python
import math
import jax
import jax.numpy as jnp
from jax import lax

G = 2048
MB = 3
SLIDES_MB = 4
CELLS_MB = 4096
SPOTS_MB = 2048


def slide_cuts(key, total):
    unit = total // (SLIDES_MB * 4)
    chosen = jax.random.permutation(key, SLIDES_MB * 4 - 1)[:SLIDES_MB - 1] + 1
    return (jnp.sort(chosen) * unit).astype(jnp.int32)


def slide_ids(cuts, total):
    position = jnp.arange(total, dtype=jnp.int32)
    return jnp.sum((position[:, None] >= cuts[None, :]).astype(jnp.int32), axis=1)


def draw_spot_slide(key, part):
    rows = [slide_ids(slide_cuts(jax.random.fold_in(key, 11 + micro), SPOTS_MB), SPOTS_MB) + micro * SLIDES_MB for micro in range(MB)]
    return jnp.stack(rows).astype(jnp.int32)


def draw_cell_slide(key, part):
    rows = [slide_ids(slide_cuts(jax.random.fold_in(key, 31 + micro), CELLS_MB), CELLS_MB) + micro * SLIDES_MB for micro in range(MB)]
    return jnp.stack(rows).astype(jnp.int32)


def draw_cell_valid(key, part):
    rows = []
    for micro in range(MB):
        cuts = slide_cuts(jax.random.fold_in(key, 31 + micro), CELLS_MB)
        position = jnp.arange(CELLS_MB, dtype=jnp.int32)
        starts = (position == 0) | jnp.any(position[:, None] == cuts[None, :], axis=1)
        coins = jax.random.randint(jax.random.fold_in(key, 61 + micro), (CELLS_MB,), 0, 12) < 11
        rows.append((coins | starts).astype(jnp.int32))
    return jnp.stack(rows)


def draw_gene_mask(key, part):
    coins = jax.random.randint(jax.random.fold_in(key, 91), (MB * SLIDES_MB, G), 0, 4) < 3
    column = jnp.arange(G, dtype=jnp.int32)[None, :]
    row_index = jnp.arange(MB * SLIDES_MB, dtype=jnp.int32)[:, None]
    return (coins | (column == row_index % G)).astype(jnp.int32)


def levels(rng, shape, cuts, least, top_value):
    level = 1.0
    for dim, parts in cuts:
        heights = jax.random.uniform(jax.random.fold_in(jax.random.fold_in(rng, 6), dim), (parts,), jnp.float32, least / len(cuts), top_value / len(cuts))
        level = level * jnp.repeat(jnp.exp(heights), shape[dim] // parts).reshape((-1,) + (1,) * (len(shape) - 1 - dim))
    return level


def normal_values(rng, extent, width, bound, split=(), held_as=jnp.bfloat16):
    level = levels(rng, extent, split, -0.22, 0.18) if split else 1.0
    array = jax.random.normal(rng, extent, jnp.float32) * width * level
    return jnp.minimum(jnp.maximum(array, -bound), bound).astype(held_as)


def setup_inputs(seed: int = 0) -> dict:
    streams_of = jax.random.split(jax.random.key(seed), 8)
    return {
        "logits": normal_values(streams_of[0], (MB, CELLS_MB, SPOTS_MB), 1.5, 8.0, ((1, 8), (2, 4)), jnp.float32),
        "expression": jnp.clip(jnp.exp(math.log(5.0) - 4.6051702 * jax.random.uniform(streams_of[1], (MB, CELLS_MB, G), jnp.float32) ** levels(streams_of[1], (MB, CELLS_MB, G), ((1, 8), (2, 4)), -0.2, 0.2)), 0.05, 5.0),
        "measured": jnp.clip(jnp.exp(math.log(5.0) - 4.6051702 * jax.random.uniform(streams_of[2], (MB, SPOTS_MB, G), jnp.float32) ** levels(streams_of[2], (MB, SPOTS_MB, G), ((1, 4), (2, 8)), -0.2, 0.2)), 0.05, 5.0),
        "spot_slide": draw_spot_slide(jax.random.fold_in(streams_of[7], 71), 0),
        "cell_slide": draw_cell_slide(jax.random.fold_in(streams_of[7], 71), 0),
        "cell_valid": draw_cell_valid(jax.random.fold_in(streams_of[7], 71), 0),
        "gene_mask": draw_gene_mask(jax.random.fold_in(streams_of[7], 71), 0),
    }


highest = lax.Precision.HIGHEST
fill_value = -1e+30
epsilon = 1e-06

@jax.custom_vjp
def low(v):
    return lax.optimization_barrier(v.astype(jnp.bfloat16)).astype(jnp.float32)

@jax.custom_vjp
def low_back(v):
    return v

def low_keep(v):
    return (low(v), None)

def low_pass(kept, grad):
    return (grad,)

def back_keep(v):
    return (v, None)

def back_low(kept, grad):
    return (low(grad),)
low.defvjp(low_keep, low_pass)
low_back.defvjp(back_keep, back_low)

def product(left, right):
    return jnp.dot(left, right, precision=highest, preferred_element_type=jnp.float32)

def forward(logits, expression, measured, spot_slide, cell_slide, cell_valid, gene_mask):
    gene_count = lax.optimization_barrier(jnp.sum(gene_mask.astype(jnp.float32), axis=1))
    loss_list, pred_list, gene_list, spot_list = ([], [], [], [])
    for micro in range(MB):
        allowed = (cell_valid[micro][:, None] == 1) & (cell_slide[micro][:, None] == spot_slide[micro][None, :])
        masked = jnp.where(allowed, logits[micro], jnp.float32(fill_value))
        column_max = lax.optimization_barrier(jnp.max(masked, axis=0, keepdims=True))
        raised = jnp.exp(masked - column_max)
        mapping = raised / lax.optimization_barrier(jnp.sum(raised, axis=0, keepdims=True))
        predicted = product(mapping.T, expression[micro])
        true_block = measured[micro]
        slide_index = jnp.arange(SLIDES_MB, dtype=jnp.int32)
        onehot = ((spot_slide[micro] - micro * SLIDES_MB)[None, :] == slide_index[:, None]).astype(jnp.float32)
        pred_sq = product(onehot, predicted * predicted)
        pred_true = product(onehot, predicted * true_block)
        true_sq = product(onehot, true_block * true_block)
        gene_cos = pred_true * lax.rsqrt(pred_sq * true_sq + epsilon)
        slide_mask = gene_mask[micro * SLIDES_MB:(micro + 1) * SLIDES_MB].astype(jnp.float32)
        counts = gene_count[micro * SLIDES_MB:(micro + 1) * SLIDES_MB]
        gene_term = jnp.sum(slide_mask * gene_cos / counts[:, None]) / SLIDES_MB
        spot_mask = product(onehot.T, slide_mask)
        spot_pp = lax.optimization_barrier(jnp.sum(spot_mask * predicted * predicted, axis=1))
        spot_pt = lax.optimization_barrier(jnp.sum(spot_mask * predicted * true_block, axis=1))
        spot_tt = lax.optimization_barrier(jnp.sum(spot_mask * true_block * true_block, axis=1))
        spot_cos = spot_pt * lax.rsqrt(spot_pp * spot_tt + epsilon)
        loss_list.append(-(gene_term + jnp.mean(spot_cos)))
        pred_list.append(predicted)
        gene_list.append(gene_cos)
        spot_list.append(spot_cos)
    return (jnp.stack(loss_list), jnp.stack(pred_list), jnp.stack(gene_list), jnp.stack(spot_list))

def reference(logits, expression, measured, spot_slide, cell_slide, cell_valid, gene_mask):

    def objective(logit_in, expression_in):
        results = forward(logit_in, expression_in, measured, spot_slide, cell_slide, cell_valid, gene_mask)
        return (CELLS_MB * jnp.sum(results[0]), results)
    value, pullback, results = jax.vjp(objective, logits, expression, has_aux=True)
    logit_grad, expression_grad = pullback(jnp.ones_like(value))
    return (results[0], results[1], results[2], results[3], logit_grad, expression_grad)
```

```python
import jax
import jax.numpy as jnp
from jax import lax
from jax.sharding import PartitionSpec as P

epsilon = 1e-06


def dot(left, right, dims):
    return lax.dot_general(
        left,
        right,
        (dims, ((), ())),
        precision=lax.Precision.HIGH,
        preferred_element_type=jnp.float32,
    )


def small_dot(left, right):
    return jnp.dot(
        left, right, precision=lax.Precision.HIGHEST, preferred_element_type=jnp.float32
    )


def cycle(count):
    wide = 1
    while 2 * (wide * 2) ** 2 <= count and count % (wide * 2) == 0:
        wide *= 2
    deep = count // wide
    if wide == 1 or deep % 2:
        return list(range(count))
    walk = []
    for row in range(deep):
        columns = range(1, wide)
        walk += [row * wide + c for c in (columns if row % 2 == 0 else reversed(columns))]
    return walk + [row * wide for row in reversed(range(deep))]


def per_device(logits, expression, measured, spot_slide, cell_slide, cell_valid, gene_mask):
    n_spot = lax.axis_size("spot")
    n_cell = lax.axis_size("cell")
    micro_count, cell_rows, spot_cols = logits.shape
    genes_cell = measured.shape[2]
    ratio = expression.shape[2] // genes_cell
    slides = gene_mask.shape[0] // micro_count
    cells_total = cell_rows * n_cell
    spots_total = spot_cols * n_spot
    spot_first = (lax.axis_index("spot") == 0).astype(jnp.float32)
    cell_first = (lax.axis_index("cell") == 0).astype(jnp.float32)
    cell_here = lax.axis_index("cell")
    gene_start = cell_here * genes_cell
    ring = cycle(n_cell)
    place = [ring.index(c) for c in range(n_cell)]
    here = jnp.asarray(place, jnp.int32)[cell_here]
    ring_table = jnp.asarray(ring, jnp.int32)
    half = n_cell // 2
    rows_half = spot_cols // 2
    forth = [(ring[q], ring[(q + 1) % n_cell]) for q in range(n_cell)]
    back = [(b, a) for a, b in forth]

    def owner(step):
        return ring_table[(here + step) % n_cell]

    def right(value):
        return lax.ppermute(value, "cell", forth)

    def left(value):
        return lax.ppermute(value, "cell", back)

    def gene_block(full, index):
        start = (index // ratio, 0, (index % ratio) * genes_cell)
        return lax.dynamic_slice(full, start, (1, cell_rows, genes_cell))[0]

    gene_count = jnp.sum(gene_mask.astype(jnp.float32), axis=1)
    slide_index = jnp.arange(slides, dtype=jnp.int32)
    allowed = (cell_valid[:, :, None] == 1) & (cell_slide[:, :, None] == spot_slide[:, None, :])
    raised = jnp.where(allowed, jnp.exp(logits), 0.0)
    inverse = 1.0 / lax.psum(jnp.sum(raised, axis=1), "cell")

    loss_list, pred_list, gene_list, spot_list, logit_list, expr_list = ([], [], [], [], [], [])
    for micro in range(micro_count):
        weights = raised[micro]
        full = lax.all_gather(expression[micro], "spot")

        def part(step):
            return dot(weights, gene_block(full, owner(step)), ((0,), (0,)))

        first = part(half)
        a = right(first[:rows_half])
        b = left(first[rows_half:])
        for k in range(half - 1, 0, -1):
            pr, pl = part(k), part(-k)
            if k == half - 1:
                pr = jnp.concatenate([pr[:rows_half] + a, pr[rows_half:]])
                pl = jnp.concatenate([pl[:rows_half], pl[rows_half:] + b])
            else:
                pr, pl = pr + a, pl + b
            a, b = right(pr), left(pl)
        own = part(0)
        predicted = (own + a + b) * inverse[micro][:, None]
        true_block = measured[micro]
        onehot = ((spot_slide[micro] - micro * slides)[None, :] == slide_index[:, None]).astype(
            jnp.float32
        )
        pred_sq, pred_true, true_sq = lax.psum(
            (
                small_dot(onehot, predicted * predicted),
                small_dot(onehot, predicted * true_block),
                small_dot(onehot, true_block * true_block),
            ),
            "spot",
        )
        gene_scale = lax.rsqrt(pred_sq * true_sq + epsilon)
        gene_cos = pred_true * gene_scale
        slide_mask = gene_mask[micro * slides : (micro + 1) * slides].astype(jnp.float32)
        local_mask = lax.dynamic_slice_in_dim(slide_mask, gene_start, genes_cell, 1)
        weight = local_mask / (slides * gene_count[micro * slides : (micro + 1) * slides][:, None])
        gene_part = jnp.sum(weight * gene_cos) * spot_first
        spot_mask = small_dot(onehot.T, local_mask)
        first_coef = small_dot(onehot.T, weight * gene_scale)
        second_coef = small_dot(onehot.T, weight * pred_true * true_sq * gene_scale**3)
        gene_grad = first_coef * true_block - second_coef * predicted
        spot_pp, spot_pt, spot_tt, gene_dot = lax.psum(
            (
                jnp.sum(spot_mask * predicted * predicted, axis=1),
                jnp.sum(spot_mask * predicted * true_block, axis=1),
                jnp.sum(spot_mask * true_block * true_block, axis=1),
                jnp.sum(gene_grad * predicted, axis=1),
            ),
            "cell",
        )
        spot_scale = lax.rsqrt(spot_pp * spot_tt + epsilon)
        spot_cos = spot_pt * spot_scale
        spot_part = jnp.sum(spot_cos) / spots_total * cell_first
        loss_list.append(-(gene_part + spot_part))
        spot_coef = spot_pt * spot_tt * spot_scale**3
        spot_grad = (
            spot_mask
            * (true_block * spot_scale[:, None] - spot_coef[:, None] * predicted)
            / spots_total
        )
        pred_grad = -cells_total * (gene_grad + spot_grad)
        centre = -cells_total * (
            gene_dot + (spot_pt * spot_scale - spot_coef * spot_pp) / spots_total
        )
        mapping = weights * inverse[micro][None, :]

        blocks = [(0, pred_grad)]
        a = b = pred_grad
        for k in range(1, half):
            a, b = right(a), left(b)
            blocks += [(-k, a), (k, b)]
        a, b = right(a[:rows_half]), left(b[rows_half:])
        blocks.append((half, jnp.concatenate([a, b])))
        mapping_grad = 0.0
        placed = jnp.zeros((n_spot, cell_rows, expression.shape[2]), jnp.float32)
        for step, block in blocks:
            index = owner(step)
            mapping_grad = mapping_grad + dot(gene_block(full, index), block, ((1,), (1,)))
            placed = lax.dynamic_update_slice(
                placed,
                dot(mapping, block, ((1,), (0,)))[None],
                (index // ratio, 0, (index % ratio) * genes_cell),
            )
        expr_list.append(lax.psum_scatter(placed, "spot", scatter_dimension=0))
        logit_list.append(mapping * (mapping_grad - centre[None, :]))
        pred_list.append(predicted)
        gene_list.append(gene_cos)
        spot_list.append(spot_cos)
    losses = lax.psum(jnp.stack(loss_list), ("spot", "cell"))
    return (
        losses,
        jnp.stack(pred_list),
        jnp.stack(gene_list),
        jnp.stack(spot_list),
        jnp.stack(logit_list),
        jnp.stack(expr_list),
    )


def solution(mesh):
    return jax.shard_map(
        per_device,
        mesh=mesh,
        in_specs=(
            P(None, "cell", "spot"),
            P(None, "cell", "spot"),
            P(None, "spot", "cell"),
            P(None, "spot"),
            P(None, "cell"),
            P(None, "cell"),
            P(),
        ),
        out_specs=(
            P(),
            P(None, "spot", "cell"),
            P(None, None, "cell"),
            P(None, "spot"),
            P(None, "cell", "spot"),
            P(None, "cell", "spot"),
        ),
        check_vma=False,
    )
```
